32 devices in a mesh: sweep: 2 (over x), na: 16 (over z, y, core).
Axes of the slice: x: 2, y: 2, z: 4, core: 2. Of those that a mesh axis runs over, the one named last changes fastest.
Arguments:
- hierarchy: float32 [32, 16, 2, 128, 128], P(('sweep', 'na')), parts along dimension 0, may hold values from -6 to 6
- hamiltonian: float32 [128, 128], replicated, may hold values from -0.5 to 0.5
- couplings: float32 [2, 128, 128], replicated, may hold values from -0.5 to 0.5
- damp_rates: float32 [4], P('sweep'), parts along dimension 0, may hold values from 0.5 to 2
- coef_real: float32 [4], P('sweep'), parts along dimension 0, may hold values from 0.5 to 2
- coef_imag: float32 [4], P('sweep'), parts along dimension 0, may hold values from -1 to 1
Outputs:
- evolved: float32 [32, 16, 2, 128, 128], P(('sweep', 'na')), parts along dimension 0
The draws below stay inside these ranges and needn't reach their ends.
There are 2 independent parts, one for each index of `sweep`. The reference program is written for one: setup_inputs(seed, part) draws one part's arguments, and reference() takes and returns one part's arrays. A program takes and returns all parts, laid end to end along the dimension named above; an argument that names none is the same for every part. Nothing has to cross between parts.
All inputs are finite; a program needn't handle non-finite values.
Results may differ from the reference program's by a relative error of at most 0.0001.
Values sent between devices are 32-bit elements; how exact they have to be, the bound alone decides.
A program may use at most 128 MiB of HBM per device.

```python
import math
import jax
import jax.numpy as jnp
from jax import lax

M = 128
STEPS = 1
N_NA = 16


def shard_levels(own_key, dims, shards, least, top_value):
    factor_of, own = 1.0, jax.random.fold_in(own_key, 6)
    for dim, parts in shards:
        heights = jnp.exp(jax.random.uniform(jax.random.fold_in(own, dim), (parts,), jnp.float32, least / len(shards), top_value / len(shards)))
        factor_of = factor_of * jnp.repeat(heights, dims[dim] // parts).reshape([-1 if axis == dim else 1 for axis in range(len(dims))])
    return factor_of


def normal_values(key, dims, width, most, shards=(), held_as=jnp.bfloat16):
    gain = shard_levels(key, dims, shards, -0.22, 0.18) if shards else 1.0
    drawn = jax.random.normal(key, dims, jnp.float32) * width * gain
    return jnp.minimum(jnp.maximum(drawn, -most), most).astype(held_as)


def setup_inputs(seed: int = 0, part: int = 0) -> dict:
    splits = jax.random.split(jax.random.key(seed), 7)
    part_splits = jax.random.split(jax.random.fold_in(splits[6], part), 7)
    hierarchy = normal_values(part_splits[0], (N_NA, N_NA, 2, M, M), 1.0, 6.0, ((0, 16),), jnp.float32)
    hamiltonian = normal_values(splits[1], (M, M), M ** -0.5, 0.5, (), jnp.float32)
    couplings = normal_values(splits[2], (2, M, M), M ** -0.5, 0.5, (), jnp.float32)
    damp_rates = jnp.clip(jnp.exp(jax.random.uniform(part_splits[3], (2,), jnp.float32, math.log(0.5), math.log(2.0))), 0.5, 2.0)
    coef_real = jnp.clip(jnp.exp(jax.random.uniform(part_splits[4], (2,), jnp.float32, math.log(0.5), math.log(2.0))), 0.5, 2.0)
    coef_imag = jnp.clip(jax.random.uniform(part_splits[5], (2,), jnp.float32, -1.0, 1.0), -1.0, 1.0)
    return dict(hierarchy=hierarchy, hamiltonian=hamiltonian, couplings=couplings, damp_rates=damp_rates, coef_real=coef_real, coef_imag=coef_imag)


step_size = 0.02

def evolve(values, raise_one, lower_one, raise_two, lower_two, first_mode, second_mode, alive_mask, hamilton, coupled, damp_rates, coef_real, coef_imag):
    matrix_order = values.shape[-1]
    magnitude = jnp.sqrt(coef_real * coef_real + coef_imag * coef_imag)
    left_terms = [values]
    right_terms = [values]
    mode_terms = ((raise_one, lower_one, first_mode), (raise_two, lower_two, second_mode))
    for which_mode in range(2):
        raised, lowered, occupied = mode_terms[which_mode]
        raise_weight = jnp.sqrt((occupied + 1.0) * magnitude[which_mode])[..., None, None]
        lower_weight = jnp.sqrt(occupied / magnitude[which_mode])[..., None, None]
        real_coef = coef_real[which_mode]
        imag_coef = coef_imag[which_mode]
        shared_re = raise_weight * raised[..., 0, :, :]
        shared_im = raise_weight * raised[..., 1, :, :]
        direct_re = lower_weight * (real_coef * lowered[..., 0, :, :])
        direct_im = lower_weight * (real_coef * lowered[..., 1, :, :])
        cross_re = lower_weight * (imag_coef * lowered[..., 1, :, :])
        cross_im = lower_weight * (imag_coef * lowered[..., 0, :, :])
        left_terms.append(jnp.stack([shared_re + direct_re - cross_re, shared_im + direct_im + cross_im], axis=-3))
        right_terms.append(jnp.stack([shared_re + direct_re + cross_re, shared_im + direct_im - cross_im], axis=-3))
    operators = (hamilton, coupled[0], coupled[1])
    flat_shape = (-1, 2, matrix_order, matrix_order)
    left_sum = sum((jnp.einsum('ab,scbd->scad', operand, stacked.reshape(flat_shape), precision=lax.Precision.HIGHEST) for operand, stacked in zip(operators, left_terms)))
    right_sum = sum((jnp.einsum('scab,bd->scad', stacked.reshape(flat_shape), operand, precision=lax.Precision.HIGHEST) for operand, stacked in zip(operators, right_terms)))
    damping = (first_mode * damp_rates[0] + second_mode * damp_rates[1]).reshape((-1, 1, 1))
    flat_values = values.reshape(flat_shape)
    change_re = left_sum[:, 1] - right_sum[:, 1] - damping * flat_values[:, 0]
    change_im = right_sum[:, 0] - left_sum[:, 0] - damping * flat_values[:, 1]
    change = jnp.stack([change_re, change_im], axis=1).reshape(values.shape)
    return change * alive_mask[..., None, None, None]

def reference(hierarchy, hamiltonian, couplings, damp_rates, coef_real, coef_imag):
    total_slots = hierarchy.shape[0]
    hamilton = 0.5 * (hamiltonian + hamiltonian.T)
    coupled = 0.5 * (couplings + jnp.swapaxes(couplings, 1, 2))
    slot_index = jnp.arange(total_slots)
    first_mode = jnp.broadcast_to(slot_index[:, None], (total_slots, total_slots)).astype(jnp.float32)
    second_mode = jnp.broadcast_to(slot_index[None, :], (total_slots, total_slots)).astype(jnp.float32)
    alive_mask = (first_mode + second_mode <= total_slots - 1).astype(jnp.float32)

    def derivative(values):
        pad_first = jnp.zeros_like(values[:1])
        pad_second = jnp.zeros_like(values[:, :1])
        raise_one = jnp.concatenate([values[1:], pad_first], 0)
        lower_one = jnp.concatenate([pad_first, values[:-1]], 0)
        raise_two = jnp.concatenate([values[:, 1:], pad_second], 1)
        lower_two = jnp.concatenate([pad_second, values[:, :-1]], 1)
        return evolve(values, raise_one, lower_one, raise_two, lower_two, first_mode, second_mode, alive_mask, hamilton, coupled, damp_rates, coef_real, coef_imag)
    values = hierarchy * alive_mask[..., None, None, None]
    for step_index in range(STEPS):
        middle = values + 0.5 * step_size * derivative(values)
        values = values + step_size * derivative(middle)
    return values
```

```python
import functools
import jax
import jax.numpy as jnp
from jax import lax
from jax.experimental import pallas as pl
from jax.experimental.pallas import tpu as pltpu
from jax.sharding import PartitionSpec as P

step_size = 0.02
MESH = pl.DeviceIdType.MESH
NEAR, OWN, PARTNER, FAR = 0, 1, 2, 3
STRIP = 32


def split(x):
    high = x.astype(jnp.bfloat16)
    return high, (x - high.astype(jnp.float32)).astype(jnp.bfloat16)


def kernel(
    total,
    order,
    hier_ref,
    ham_ref,
    coup_ref,
    damp_ref,
    creal_ref,
    cimag_ref,
    out_ref,
    rho,
    mid,
    w_left,
    w_right,
    x_left,
    x_right,
    table,
    own_sem,
    send_sem,
    recv_sem,
):
    M, N = order, total
    p = lax.axis_index("na")
    chip = p // 2
    core = p % 2
    odd = chip % 2
    chips = N // 2
    first = core == 0
    K = N - p
    pairs = N - 1 - 2 * chip

    is_relay = core != odd
    relays = jnp.logical_and(
        is_relay, jnp.where(odd == 1, chip >= 2, chip + 2 < chips)
    )
    fed_by_relay = jnp.logical_and(
        core == odd, jnp.where(odd == 1, chip + 2 < chips, chip >= 2)
    )
    direct_to = jnp.where(odd == 1, 2 * chip - 1, 2 * chip + 2)
    relay_to = jnp.where(odd == 1, p - 3, p + 3)
    relay_from = jnp.where(odd == 1, p + 3, p - 3)

    direct_count = jnp.where(p == 0, K - 2, K)
    near_count = jnp.where(first, jnp.where(p == 0, 0, K + 1), K - 1)
    far_count = jnp.where(
        first,
        jnp.where(
            p == 0, 0, jnp.where(jnp.logical_and(odd == 1, chip >= 2), K + 2, K)
        ),
        jnp.maximum(K - 2, 0),
    )
    relay_near_count = jnp.where(relays, jnp.where(first, near_count, K - 3), 0)
    relay_far_count = jnp.where(relays, far_count, 0)
    mid_near_count = jnp.where(first, jnp.where(p == 0, 0, K), K - 1)
    direct_slot = jnp.where(core == odd, FAR, NEAR)

    def own_copy(i):
        return pltpu.make_async_copy(
            hier_ref.at[0, i], rho.at[OWN, i], own_sem.at[i]
        )

    def remote(src, dst, send, recv, i, target):
        return pltpu.make_async_remote_copy(
            src_ref=src,
            dst_ref=dst,
            send_sem=send_sem.at[send, i],
            recv_sem=recv_sem.at[recv, i],
            device_id={"na": target},
            device_id_type=MESH,
        )

    def direct_copy(i):
        return remote(
            hier_ref.at[0, i], rho.at[direct_slot, i], 0, direct_slot, i, direct_to
        )

    def partner_copy(i):
        return remote(
            hier_ref.at[0, i], rho.at[PARTNER, i], 1, PARTNER, i, p + 1 - 2 * core
        )

    def relay_near(i):
        return remote(rho.at[NEAR, i], rho.at[FAR, i], 2, FAR, i, relay_to)

    def relay_far(i):
        return remote(rho.at[FAR, i], rho.at[NEAR, i], 3, NEAR, i, relay_to)

    def mid_copy(i):
        return remote(
            mid.at[OWN, i], mid.at[PARTNER, i], 4, 1, i, p + 1 - 2 * core
        )

    def arrival(which, i):
        return remote(
            rho.at[which, i], rho.at[which, i], 0, which, i, p + 1 - 2 * core
        )

    @pl.loop(0, K)
    def _(i):
        own_copy(i).start()

    barrier = pltpu.get_barrier_semaphore()

    def greet(target):
        pl.semaphore_signal(
            barrier, inc=1, device_id={"na": target}, device_id_type=MESH
        )

    greet(p + 1 - 2 * core)
    greet(direct_to)

    @pl.when(is_relay)
    def _():
        greet(jnp.where(odd == 1, p - 2, p + 2))

    @pl.when(relays)
    def _():
        greet(relay_to)

    @pl.when(fed_by_relay)
    def _():
        greet(relay_from)

    pl.semaphore_wait(
        barrier,
        2
        + is_relay.astype(jnp.int32)
        + relays.astype(jnp.int32)
        + fed_by_relay.astype(jnp.int32),
    )

    @pl.loop(0, K)
    def _(i):
        @pl.when(i < direct_count)
        def _():
            direct_copy(i).start()

        @pl.when(i < pairs)
        def _():
            partner_copy(i).start()

    for k in range(3):
        raw = ham_ref[...] if k == 0 else coup_ref[k - 1]
        high, low = split(0.5 * (raw + raw.T))
        for half in range(2):
            cols = slice((3 * half + k) * M, (3 * half + k + 1) * M)
            w_left[0:M, cols] = high
            w_left[M : 2 * M, cols] = low
            w_right[cols, 0:M] = high
            w_right[cols, M : 2 * M] = low

    for mode in range(2):
        re = jnp.full((8, M), creal_ref[mode], jnp.float32)
        im = jnp.full((8, M), cimag_ref[mode], jnp.float32)
        magnitude = jnp.sqrt(re * re + im * im)

        @pl.loop(0, N)
        def _(n):
            occupied = jnp.full((8, M), n.astype(jnp.float32), jnp.float32)
            lower = jnp.sqrt(occupied / magnitude)
            table[3 * mode, n] = jnp.sqrt((occupied + 1.0) * magnitude)
            table[3 * mode + 1, n] = lower * re
            table[3 * mode + 2, n] = lower * im

    @pl.loop(K, N)
    def _(i):
        out_ref[0, i] = jnp.zeros((2, M, M), jnp.float32)

    def derivative(buf, own, up, down, q, n, base, scale, store):
        alive = q + n < N - 1
        alive_scale = jnp.where(alive, 1.0, 0.0)
        up = jnp.where(alive, up, own)
        above = jnp.where(alive, n + 1, n)
        below = jnp.maximum(n - 1, 0)
        terms = []
        for mode, occupied in ((0, q), (1, n)):
            terms.append(
                (
                    table[3 * mode, occupied, 0:1, :] * alive_scale,
                    table[3 * mode + 1, occupied, 0:1, :],
                    table[3 * mode + 2, occupied, 0:1, :],
                )
            )
        sources = (((up, n), (down, n)), ((own, above), (own, below)))

        def put(block, rows, part, left, right):
            for x, is_left in ((left, True), (right, False)):
                high, low = split(x)
                for half, value in ((0, high), (1, low)):
                    at = (3 * half + block) * M
                    if is_left:
                        x_left[
                            at + rows : at + rows + STRIP, part * M : (part + 1) * M
                        ] = value
                    else:
                        x_right[
                            part * M + rows : part * M + rows + STRIP, at : at + M
                        ] = value

        for rows in range(0, M, STRIP):
            strip = slice(rows, rows + STRIP)
            for part in range(2):
                high, low = split(buf[own, n, part, strip, :])
                for half, value in ((0, high), (1, low)):
                    at = 3 * half * M
                    x_left[
                        at + rows : at + rows + STRIP, part * M : (part + 1) * M
                    ] = value
                    x_right[
                        part * M + rows : part * M + rows + STRIP, at : at + M
                    ] = value
            for mode in range(2):
                raise_w, direct_w, cross_w = terms[mode]
                (ub, us), (vb, vs) = sources[mode]
                v_re = buf[vb, vs, 0, strip, :]
                v_im = buf[vb, vs, 1, strip, :]
                e_re = raise_w * buf[ub, us, 0, strip, :] + direct_w * v_re
                e_im = raise_w * buf[ub, us, 1, strip, :] + direct_w * v_im
                x_re = cross_w * v_im
                x_im = cross_w * v_re
                put(1 + mode, rows, 0, e_re - x_re, e_re + x_re)
                put(1 + mode, rows, 1, e_im + x_im, e_im - x_im)
        left = jnp.dot(w_left[...], x_left[...], preferred_element_type=jnp.float32)
        right = jnp.dot(x_right[...], w_right[...], preferred_element_type=jnp.float32)
        damping = q.astype(jnp.float32) * damp_ref[0] + n.astype(jnp.float32) * damp_ref[1]
        left = left[0:M] + left[M : 2 * M]
        right = right[:, 0:M] + right[:, M : 2 * M]
        change_re = left[:, M : 2 * M] - right[M : 2 * M] - damping * buf[own, n, 0]
        change_im = right[0:M] - left[:, 0:M] - damping * buf[own, n, 1]
        store(0, base(0) + scale * change_re)
        store(1, base(1) + scale * change_im)

    up = jnp.where(first, PARTNER, NEAR)
    down = jnp.where(first, jnp.where(p == 0, OWN, NEAR), PARTNER)
    near_up = jnp.where(first, OWN, FAR)
    near_down = jnp.where(first, FAR, OWN)
    near_q = jnp.where(first, p - 1, p + 1)

    def take(i):
        @pl.when(i < K)
        def _():
            own_copy(i).wait()

        @pl.when(i < near_count)
        def _():
            arrival(NEAR, i).wait_recv()

        @pl.when(i < relay_near_count)
        def _():
            relay_near(i).start()

        @pl.when(i < far_count)
        def _():
            arrival(FAR, i).wait_recv()

        @pl.when(i < relay_far_count)
        def _():
            relay_far(i).start()

    take(jnp.int32(0))

    @pl.loop(0, K + 2)
    def _(i):
        take(i + 1)

        @pl.when(i < pairs)
        def _():
            arrival(PARTNER, i).wait_recv()

        @pl.when(i < K)
        def _():
            def store(part, value):
                mid[OWN, i, part] = value

            derivative(
                rho, OWN, up, down, p, i,
                lambda part: rho[OWN, i, part], 0.5 * step_size, store,
            )

        @pl.when(i < mid_near_count)
        def _():
            def store(part, value):
                mid[NEAR, i, part] = value

            derivative(
                rho, NEAR, near_up, near_down, near_q, i,
                lambda part: rho[NEAR, i, part], 0.5 * step_size, store,
            )

        @pl.when(i < pairs)
        def _():
            mid_copy(i).start()

        @pl.when(i >= 2)
        def _():
            j = i - 2

            @pl.when(j < pairs)
            def _():
                mid_copy(j).wait_recv()

            def store(part, value):
                out_ref[0, j, part] = value

            derivative(
                mid, OWN, up, down, p, j,
                lambda part: rho[OWN, j, part], step_size, store,
            )

    @pl.loop(0, N)
    def _(i):
        @pl.when(i < direct_count)
        def _():
            direct_copy(i).wait_send()

        @pl.when(i < pairs)
        def _():
            partner_copy(i).wait_send()
            mid_copy(i).wait_send()

        @pl.when(i < relay_near_count)
        def _():
            relay_near(i).wait_send()

        @pl.when(i < relay_far_count)
        def _():
            relay_far(i).wait_send()


def per_device(hierarchy, hamiltonian, couplings, damp_rates, coef_real, coef_imag):
    total = hierarchy.shape[1]
    M = hierarchy.shape[-1]
    vmem = pl.BlockSpec(memory_space=pltpu.VMEM)
    smem = pl.BlockSpec(memory_space=pltpu.SMEM)
    return pl.pallas_call(
        functools.partial(kernel, total, M),
        out_shape=jax.ShapeDtypeStruct(hierarchy.shape, jnp.float32),
        in_specs=[pl.BlockSpec(memory_space=pl.ANY), vmem, vmem, smem, smem, smem],
        out_specs=vmem,
        scratch_shapes=[
            pltpu.VMEM((4, total, 2, M, M), jnp.float32),
            pltpu.VMEM((3, total, 2, M, M), jnp.float32),
            pltpu.VMEM((2 * M, 6 * M), jnp.bfloat16),
            pltpu.VMEM((6 * M, 2 * M), jnp.bfloat16),
            pltpu.VMEM((6 * M, 2 * M), jnp.bfloat16),
            pltpu.VMEM((2 * M, 6 * M), jnp.bfloat16),
            pltpu.VMEM((6, total, 8, M), jnp.float32),
            pltpu.SemaphoreType.DMA((total,)),
            pltpu.SemaphoreType.DMA((5, total)),
            pltpu.SemaphoreType.DMA((4, total)),
        ],
        compiler_params=pltpu.CompilerParams(
            collective_id=0, has_side_effects=True, vmem_limit_bytes=60 * 2**20
        ),
    )(hierarchy, hamiltonian, couplings, damp_rates, coef_real, coef_imag)


def solution(mesh):
    in_specs = (
        P(("sweep", "na"), None, None, None, None),
        P(),
        P(),
        P("sweep"),
        P("sweep"),
        P("sweep"),
    )
    out_specs = P(("sweep", "na"), None, None, None, None)
    return jax.shard_map(
        per_device, mesh=mesh, in_specs=in_specs, out_specs=out_specs, check_vma=False
    )
```

```python
import functools
import jax
import jax.numpy as jnp
from jax import lax
from jax.experimental import pallas as pl
from jax.experimental.pallas import tpu as pltpu
from jax.sharding import PartitionSpec as P

step_size = 0.02
MESH = pl.DeviceIdType.MESH
NEAR, OWN, PARTNER, FAR = 0, 1, 2, 3
STRIP = 32


def split(x):
    high = x.astype(jnp.bfloat16)
    return high, (x - high.astype(jnp.float32)).astype(jnp.bfloat16)


def kernel(
    total,
    order,
    hier_ref,
    ham_ref,
    coup_ref,
    damp_ref,
    creal_ref,
    cimag_ref,
    out_ref,
    rho,
    mid,
    w_left,
    w_right,
    x_left,
    x_right,
    table,
    out_buf,
    ham_buf,
    own_sem,
    out_sem,
    ham_sem,
    send_sem,
    recv_sem,
):
    M, N = order, total
    p = lax.axis_index("na")
    chip = p // 2
    core = p % 2
    odd = chip % 2
    chips = N // 2
    first = core == 0
    K = N - p
    pairs = N - 1 - 2 * chip

    is_relay = core != odd
    relays = jnp.logical_and(
        is_relay, jnp.where(odd == 1, chip >= 2, chip + 2 < chips)
    )
    fed_by_relay = jnp.logical_and(
        core == odd, jnp.where(odd == 1, chip + 2 < chips, chip >= 2)
    )
    direct_to = jnp.where(odd == 1, 2 * chip - 1, 2 * chip + 2)
    relay_to = jnp.where(odd == 1, p - 3, p + 3)
    relay_from = jnp.where(odd == 1, p + 3, p - 3)

    direct_count = jnp.where(p == 0, K - 2, K)
    near_count = jnp.where(first, jnp.where(p == 0, 0, K + 1), K - 1)
    far_count = jnp.where(
        first,
        jnp.where(
            p == 0, 0, jnp.where(jnp.logical_and(odd == 1, chip >= 2), K + 2, K)
        ),
        jnp.maximum(K - 2, 0),
    )
    relay_near_count = jnp.where(relays, jnp.where(first, near_count, K - 3), 0)
    relay_far_count = jnp.where(relays, far_count, 0)
    mid_near_count = jnp.where(first, jnp.where(p == 0, 0, K), K - 1)
    direct_slot = jnp.where(core == odd, FAR, NEAR)

    def own_copy(i):
        return pltpu.make_async_copy(
            hier_ref.at[0, i], rho.at[OWN, i], own_sem.at[i]
        )

    def operator_copy(k):
        return pltpu.make_async_copy(
            ham_ref if k == 0 else coup_ref.at[k - 1], ham_buf.at[k], ham_sem.at[k]
        )

    def out_copy(i):
        return pltpu.make_async_copy(out_buf.at[i], out_ref.at[0, i], out_sem.at[i])

    def remote(src, dst, send, recv, i, target):
        return pltpu.make_async_remote_copy(
            src_ref=src,
            dst_ref=dst,
            send_sem=send_sem.at[send, i],
            recv_sem=recv_sem.at[recv, i],
            device_id={"na": target},
            device_id_type=MESH,
        )

    def direct_copy(i):
        return remote(
            hier_ref.at[0, i], rho.at[direct_slot, i], 0, direct_slot, i, direct_to
        )

    def partner_copy(i):
        return remote(
            hier_ref.at[0, i], rho.at[PARTNER, i], 1, PARTNER, i, p + 1 - 2 * core
        )

    def relay_near(i):
        return remote(rho.at[NEAR, i], rho.at[FAR, i], 2, FAR, i, relay_to)

    def relay_far(i):
        return remote(rho.at[FAR, i], rho.at[NEAR, i], 3, NEAR, i, relay_to)

    def mid_copy(i):
        return remote(
            mid.at[OWN, i], mid.at[PARTNER, i], 4, 1, i, p + 1 - 2 * core
        )

    def arrival(which, i):
        return remote(
            rho.at[which, i], rho.at[which, i], 0, which, i, p + 1 - 2 * core
        )

    barrier = pltpu.get_barrier_semaphore()

    def greet(target):
        pl.semaphore_signal(
            barrier, inc=1, device_id={"na": target}, device_id_type=MESH
        )

    greet(p + 1 - 2 * core)
    greet(direct_to)

    @pl.when(is_relay)
    def _():
        greet(jnp.where(odd == 1, p - 2, p + 2))

    @pl.when(relays)
    def _():
        greet(relay_to)

    @pl.when(fed_by_relay)
    def _():
        greet(relay_from)

    pl.semaphore_wait(
        barrier,
        2
        + is_relay.astype(jnp.int32)
        + relays.astype(jnp.int32)
        + fed_by_relay.astype(jnp.int32),
    )

    @pl.loop(0, K)
    def _(i):
        @pl.when(i < direct_count)
        def _():
            direct_copy(i).start()

        @pl.when(i < pairs)
        def _():
            partner_copy(i).start()

    for k in range(3):
        operator_copy(k).start()

    @pl.loop(0, K)
    def _(i):
        own_copy(i).start()

    for k in range(3):
        operator_copy(k).wait()
        raw = ham_buf[k]
        high, low = split(0.5 * (raw + raw.T))
        for half in range(2):
            cols = slice((3 * half + k) * M, (3 * half + k + 1) * M)
            w_left[0:M, cols] = high
            w_left[M : 2 * M, cols] = low
            w_right[cols, 0:M] = high
            w_right[cols, M : 2 * M] = low

    for mode in range(2):
        re = jnp.full((8, M), creal_ref[mode], jnp.float32)
        im = jnp.full((8, M), cimag_ref[mode], jnp.float32)
        magnitude = jnp.sqrt(re * re + im * im)

        @pl.loop(0, N)
        def _(n):
            occupied = jnp.full((8, M), n.astype(jnp.float32), jnp.float32)
            lower = jnp.sqrt(occupied / magnitude)
            table[3 * mode, n] = jnp.sqrt((occupied + 1.0) * magnitude)
            table[3 * mode + 1, n] = lower * re
            table[3 * mode + 2, n] = lower * im

    @pl.loop(K, N)
    def _(i):
        out_buf[i] = jnp.zeros((2, M, M), jnp.float32)

    def derivative(buf, own, up, down, q, n, base, scale, store):
        alive = q + n < N - 1
        alive_scale = jnp.where(alive, 1.0, 0.0)
        up = jnp.where(alive, up, own)
        above = jnp.where(alive, n + 1, n)
        below = jnp.maximum(n - 1, 0)
        terms = []
        for mode, occupied in ((0, q), (1, n)):
            terms.append(
                (
                    table[3 * mode, occupied, 0:1, :] * alive_scale,
                    table[3 * mode + 1, occupied, 0:1, :],
                    table[3 * mode + 2, occupied, 0:1, :],
                )
            )
        sources = (((up, n), (down, n)), ((own, above), (own, below)))

        def put(block, rows, part, left, right):
            for x, is_left in ((left, True), (right, False)):
                high, low = split(x)
                for half, value in ((0, high), (1, low)):
                    at = (3 * half + block) * M
                    if is_left:
                        x_left[
                            at + rows : at + rows + STRIP, part * M : (part + 1) * M
                        ] = value
                    else:
                        x_right[
                            part * M + rows : part * M + rows + STRIP, at : at + M
                        ] = value

        for rows in range(0, M, STRIP):
            strip = slice(rows, rows + STRIP)
            for part in range(2):
                high, low = split(buf[own, n, part, strip, :])
                for half, value in ((0, high), (1, low)):
                    at = 3 * half * M
                    x_left[
                        at + rows : at + rows + STRIP, part * M : (part + 1) * M
                    ] = value
                    x_right[
                        part * M + rows : part * M + rows + STRIP, at : at + M
                    ] = value
            for mode in range(2):
                raise_w, direct_w, cross_w = terms[mode]
                (ub, us), (vb, vs) = sources[mode]
                v_re = buf[vb, vs, 0, strip, :]
                v_im = buf[vb, vs, 1, strip, :]
                e_re = raise_w * buf[ub, us, 0, strip, :] + direct_w * v_re
                e_im = raise_w * buf[ub, us, 1, strip, :] + direct_w * v_im
                x_re = cross_w * v_im
                x_im = cross_w * v_re
                put(1 + mode, rows, 0, e_re - x_re, e_re + x_re)
                put(1 + mode, rows, 1, e_im + x_im, e_im - x_im)
        left = jnp.dot(w_left[...], x_left[...], preferred_element_type=jnp.float32)
        right = jnp.dot(x_right[...], w_right[...], preferred_element_type=jnp.float32)
        damping = q.astype(jnp.float32) * damp_ref[0] + n.astype(jnp.float32) * damp_ref[1]
        left = left[0:M] + left[M : 2 * M]
        right = right[:, 0:M] + right[:, M : 2 * M]
        change_re = left[:, M : 2 * M] - right[M : 2 * M] - damping * buf[own, n, 0]
        change_im = right[0:M] - left[:, 0:M] - damping * buf[own, n, 1]
        store(0, base(0) + scale * change_re)
        store(1, base(1) + scale * change_im)

    up = jnp.where(first, PARTNER, NEAR)
    down = jnp.where(first, jnp.where(p == 0, OWN, NEAR), PARTNER)
    near_up = jnp.where(first, OWN, FAR)
    near_down = jnp.where(first, FAR, OWN)
    near_q = jnp.where(first, p - 1, p + 1)

    def take_own(i):
        @pl.when(i < K)
        def _():
            own_copy(i).wait()

    def take(i):
        @pl.when(i < near_count)
        def _():
            arrival(NEAR, i).wait_recv()

        @pl.when(i < relay_near_count)
        def _():
            relay_near(i).start()

        @pl.when(i < far_count)
        def _():
            arrival(FAR, i).wait_recv()

        @pl.when(i < relay_far_count)
        def _():
            relay_far(i).start()

    def middle(which, i, up, down, q):
        def store(part, value):
            mid[which, i, part] = value

        derivative(
            rho, which, up, down, q, i,
            lambda part: rho[which, i, part], 0.5 * step_size, store,
        )

    take_own(jnp.int32(0))

    @pl.loop(K, N)
    def _(i):
        out_copy(i).start()

    @pl.loop(-1, K)
    def _(i):
        take_own(i + 2)
        take(i + 1)

        @pl.when(i + 1 < pairs)
        def _():
            arrival(PARTNER, i + 1).wait_recv()

        @pl.when(i + 1 < K)
        def _():
            middle(OWN, i + 1, up, down, p)

        @pl.when(jnp.logical_and(i >= 0, i < mid_near_count))
        def _():
            middle(NEAR, i, near_up, near_down, near_q)

        @pl.when(i + 1 < pairs)
        def _():
            mid_copy(i + 1).start()

        @pl.when(i >= 1)
        def _():
            out_copy(i - 1).start()

        @pl.when(i >= 0)
        def _():
            @pl.when(i < pairs)
            def _():
                mid_copy(i).wait_recv()

            def store(part, value):
                out_buf[i, part] = value

            derivative(
                mid, OWN, up, down, p, i,
                lambda part: rho[OWN, i, part], step_size, store,
            )

    take(K + 1)

    out_copy(K - 1).start()

    @pl.loop(0, N)
    def _(i):
        @pl.when(i < direct_count)
        def _():
            direct_copy(i).wait_send()

        @pl.when(i < pairs)
        def _():
            partner_copy(i).wait_send()
            mid_copy(i).wait_send()

        @pl.when(i < relay_near_count)
        def _():
            relay_near(i).wait_send()

        @pl.when(i < relay_far_count)
        def _():
            relay_far(i).wait_send()

        out_copy(i).wait()


def per_device(hierarchy, hamiltonian, couplings, damp_rates, coef_real, coef_imag):
    total = hierarchy.shape[1]
    M = hierarchy.shape[-1]
    hbm = pl.BlockSpec(memory_space=pltpu.HBM)
    smem = pl.BlockSpec(memory_space=pltpu.SMEM)
    return pl.pallas_call(
        functools.partial(kernel, total, M),
        out_shape=jax.ShapeDtypeStruct(hierarchy.shape, jnp.float32),
        in_specs=[hbm] * 3 + [smem] * 3,
        out_specs=pl.BlockSpec(memory_space=pl.ANY),
        scratch_shapes=[
            pltpu.VMEM((4, total, 2, M, M), jnp.float32),
            pltpu.VMEM((3, total, 2, M, M), jnp.float32),
            pltpu.VMEM((2 * M, 6 * M), jnp.bfloat16),
            pltpu.VMEM((6 * M, 2 * M), jnp.bfloat16),
            pltpu.VMEM((6 * M, 2 * M), jnp.bfloat16),
            pltpu.VMEM((2 * M, 6 * M), jnp.bfloat16),
            pltpu.VMEM((6, total, 8, M), jnp.float32),
            pltpu.VMEM((total, 2, M, M), jnp.float32),
            pltpu.VMEM((3, M, M), jnp.float32),
            pltpu.SemaphoreType.DMA((total,)),
            pltpu.SemaphoreType.DMA((total,)),
            pltpu.SemaphoreType.DMA((3,)),
            pltpu.SemaphoreType.DMA((5, total)),
            pltpu.SemaphoreType.DMA((4, total)),
        ],
        compiler_params=pltpu.CompilerParams(
            collective_id=0, has_side_effects=True, vmem_limit_bytes=(8 + total) * 2**20
        ),
    )(hierarchy, hamiltonian, couplings, damp_rates, coef_real, coef_imag)


def solution(mesh):
    in_specs = (
        P(("sweep", "na"), None, None, None, None),
        P(),
        P(),
        P("sweep"),
        P("sweep"),
        P("sweep"),
    )
    out_specs = P(("sweep", "na"), None, None, None, None)
    return jax.shard_map(
        per_device, mesh=mesh, in_specs=in_specs, out_specs=out_specs, check_vma=False
    )
```

```python
import functools
import jax
import jax.numpy as jnp
from jax import lax
from jax.experimental import pallas as pl
from jax.experimental.pallas import tpu as pltpu
from jax.sharding import PartitionSpec as P

step_size = 0.02
MESH = pl.DeviceIdType.MESH
NEAR, OWN, PARTNER, FAR = 0, 1, 2, 3
STRIP = 32


def split(x):
    high = x.astype(jnp.bfloat16)
    return high, (x - high.astype(jnp.float32)).astype(jnp.bfloat16)


def kernel(
    total,
    order,
    hier_ref,
    ham_ref,
    coup_ref,
    damp_in,
    creal_in,
    cimag_in,
    out_ref,
    rho,
    mid,
    w_left,
    w_right,
    x_left,
    x_right,
    table,
    out_buf,
    ham_buf,
    damp_ref,
    creal_ref,
    cimag_ref,
    own_sem,
    out_sem,
    ham_sem,
    small_sem,
    send_sem,
    recv_sem,
):
    M, N = order, total
    p = lax.axis_index("na")
    chip = p // 2
    core = p % 2
    odd = chip % 2
    chips = N // 2
    first = core == 0
    K = N - p
    pairs = N - 1 - 2 * chip

    is_relay = core != odd
    relays = jnp.logical_and(
        is_relay, jnp.where(odd == 1, chip >= 2, chip + 2 < chips)
    )
    fed_by_relay = jnp.logical_and(
        core == odd, jnp.where(odd == 1, chip + 2 < chips, chip >= 2)
    )
    direct_to = jnp.where(odd == 1, 2 * chip - 1, 2 * chip + 2)
    relay_to = jnp.where(odd == 1, p - 3, p + 3)
    relay_from = jnp.where(odd == 1, p + 3, p - 3)

    direct_count = jnp.where(p == 0, K - 2, K)
    near_count = jnp.where(first, jnp.where(p == 0, 0, K + 1), K - 1)
    far_count = jnp.where(
        first,
        jnp.where(
            p == 0, 0, jnp.where(jnp.logical_and(odd == 1, chip >= 2), K + 2, K)
        ),
        jnp.maximum(K - 2, 0),
    )
    relay_near_count = jnp.where(relays, jnp.where(first, near_count, K - 3), 0)
    relay_far_count = jnp.where(relays, far_count, 0)
    mid_near_count = jnp.where(first, jnp.where(p == 0, 0, K), K - 1)
    direct_slot = jnp.where(core == odd, FAR, NEAR)

    def own_copy(i):
        return pltpu.make_async_copy(
            hier_ref.at[0, i], rho.at[OWN, i], own_sem.at[i]
        )

    def operator_copy(k):
        return pltpu.make_async_copy(
            ham_ref if k == 0 else coup_ref.at[k - 1], ham_buf.at[k], ham_sem.at[k]
        )

    def out_copy(i):
        return pltpu.make_async_copy(out_buf.at[i], out_ref.at[0, i], out_sem.at[i])

    def remote(src, dst, send, recv, i, target):
        return pltpu.make_async_remote_copy(
            src_ref=src,
            dst_ref=dst,
            send_sem=send_sem.at[send, i],
            recv_sem=recv_sem.at[recv, i],
            device_id={"na": target},
            device_id_type=MESH,
        )

    def direct_copy(i):
        return remote(
            hier_ref.at[0, i], rho.at[direct_slot, i], 0, direct_slot, i, direct_to
        )

    def partner_copy(i):
        return remote(
            hier_ref.at[0, i], rho.at[PARTNER, i], 1, PARTNER, i, p + 1 - 2 * core
        )

    def relay_near(i):
        return remote(rho.at[NEAR, i], rho.at[FAR, i], 2, FAR, i, relay_to)

    def relay_far(i):
        return remote(rho.at[FAR, i], rho.at[NEAR, i], 3, NEAR, i, relay_to)

    def mid_copy(i):
        return remote(
            mid.at[OWN, i], mid.at[PARTNER, i], 4, 1, i, p + 1 - 2 * core
        )

    def arrival(which, i):
        return remote(
            rho.at[which, i], rho.at[which, i], 0, which, i, p + 1 - 2 * core
        )

    barrier = pltpu.get_barrier_semaphore()

    def greet(target):
        pl.semaphore_signal(
            barrier, inc=1, device_id={"na": target}, device_id_type=MESH
        )

    greet(p + 1 - 2 * core)
    greet(direct_to)

    @pl.when(is_relay)
    def _():
        greet(jnp.where(odd == 1, p - 2, p + 2))

    @pl.when(relays)
    def _():
        greet(relay_to)

    @pl.when(fed_by_relay)
    def _():
        greet(relay_from)

    pl.semaphore_wait(
        barrier,
        2
        + is_relay.astype(jnp.int32)
        + relays.astype(jnp.int32)
        + fed_by_relay.astype(jnp.int32),
    )

    @pl.loop(0, K)
    def _(i):
        @pl.when(i < direct_count)
        def _():
            direct_copy(i).start()

        @pl.when(i < pairs)
        def _():
            partner_copy(i).start()

    small = [
        pltpu.make_async_copy(source, target, small_sem.at[k])
        for k, (source, target) in enumerate(
            ((damp_in, damp_ref), (creal_in, creal_ref), (cimag_in, cimag_ref))
        )
    ]
    for k in range(3):
        small[k].start()
        operator_copy(k).start()

    @pl.loop(0, K)
    def _(i):
        own_copy(i).start()

    for k in range(3):
        operator_copy(k).wait()
        raw = ham_buf[k]
        high, low = split(0.5 * (raw + raw.T))
        for half in range(2):
            cols = slice((3 * half + k) * M, (3 * half + k + 1) * M)
            w_left[0:M, cols] = high
            w_left[M : 2 * M, cols] = low
            w_right[cols, 0:M] = high
            w_right[cols, M : 2 * M] = low

    for copy in small:
        copy.wait()

    for mode in range(2):
        re = jnp.full((8, M), creal_ref[mode], jnp.float32)
        im = jnp.full((8, M), cimag_ref[mode], jnp.float32)
        magnitude = jnp.sqrt(re * re + im * im)

        @pl.loop(0, N)
        def _(n):
            occupied = jnp.full((8, M), n.astype(jnp.float32), jnp.float32)
            lower = jnp.sqrt(occupied / magnitude)
            table[3 * mode, n] = jnp.sqrt((occupied + 1.0) * magnitude)
            table[3 * mode + 1, n] = lower * re
            table[3 * mode + 2, n] = lower * im

    @pl.loop(K, N)
    def _(i):
        out_buf[i] = jnp.zeros((2, M, M), jnp.float32)

    def derivative(buf, own, up, down, q, n, base, scale, store):
        alive = q + n < N - 1
        alive_scale = jnp.where(alive, 1.0, 0.0)
        up = jnp.where(alive, up, own)
        above = jnp.where(alive, n + 1, n)
        below = jnp.maximum(n - 1, 0)
        terms = []
        for mode, occupied in ((0, q), (1, n)):
            terms.append(
                (
                    table[3 * mode, occupied, 0:1, :] * alive_scale,
                    table[3 * mode + 1, occupied, 0:1, :],
                    table[3 * mode + 2, occupied, 0:1, :],
                )
            )
        sources = (((up, n), (down, n)), ((own, above), (own, below)))

        def put(block, rows, part, left, right):
            for x, is_left in ((left, True), (right, False)):
                high, low = split(x)
                for half, value in ((0, high), (1, low)):
                    at = (3 * half + block) * M
                    if is_left:
                        x_left[
                            at + rows : at + rows + STRIP, part * M : (part + 1) * M
                        ] = value
                    else:
                        x_right[
                            part * M + rows : part * M + rows + STRIP, at : at + M
                        ] = value

        for rows in range(0, M, STRIP):
            strip = slice(rows, rows + STRIP)
            for part in range(2):
                high, low = split(buf[own, n, part, strip, :])
                for half, value in ((0, high), (1, low)):
                    at = 3 * half * M
                    x_left[
                        at + rows : at + rows + STRIP, part * M : (part + 1) * M
                    ] = value
                    x_right[
                        part * M + rows : part * M + rows + STRIP, at : at + M
                    ] = value
            for mode in range(2):
                raise_w, direct_w, cross_w = terms[mode]
                (ub, us), (vb, vs) = sources[mode]
                v_re = buf[vb, vs, 0, strip, :]
                v_im = buf[vb, vs, 1, strip, :]
                e_re = raise_w * buf[ub, us, 0, strip, :] + direct_w * v_re
                e_im = raise_w * buf[ub, us, 1, strip, :] + direct_w * v_im
                x_re = cross_w * v_im
                x_im = cross_w * v_re
                put(1 + mode, rows, 0, e_re - x_re, e_re + x_re)
                put(1 + mode, rows, 1, e_im + x_im, e_im - x_im)
        left = jnp.dot(w_left[...], x_left[...], preferred_element_type=jnp.float32)
        right = jnp.dot(x_right[...], w_right[...], preferred_element_type=jnp.float32)
        damping = q.astype(jnp.float32) * damp_ref[0] + n.astype(jnp.float32) * damp_ref[1]
        left = left[0:M] + left[M : 2 * M]
        right = right[:, 0:M] + right[:, M : 2 * M]
        change_re = left[:, M : 2 * M] - right[M : 2 * M] - damping * buf[own, n, 0]
        change_im = right[0:M] - left[:, 0:M] - damping * buf[own, n, 1]
        store(0, base(0) + scale * change_re)
        store(1, base(1) + scale * change_im)

    up = jnp.where(first, PARTNER, NEAR)
    down = jnp.where(first, jnp.where(p == 0, OWN, NEAR), PARTNER)
    near_up = jnp.where(first, OWN, FAR)
    near_down = jnp.where(first, FAR, OWN)
    near_q = jnp.where(first, p - 1, p + 1)

    def take_own(i):
        @pl.when(i < K)
        def _():
            own_copy(i).wait()

    def take(i):
        @pl.when(i < near_count)
        def _():
            arrival(NEAR, i).wait_recv()

        @pl.when(i < relay_near_count)
        def _():
            relay_near(i).start()

        @pl.when(i < far_count)
        def _():
            arrival(FAR, i).wait_recv()

        @pl.when(i < relay_far_count)
        def _():
            relay_far(i).start()

    def middle(which, i, up, down, q):
        def store(part, value):
            mid[which, i, part] = value

        derivative(
            rho, which, up, down, q, i,
            lambda part: rho[which, i, part], 0.5 * step_size, store,
        )

    take_own(jnp.int32(0))

    @pl.loop(K, N)
    def _(i):
        out_copy(i).start()

    @pl.loop(-1, K)
    def _(i):
        take_own(i + 2)
        take(i + 1)

        @pl.when(i + 1 < pairs)
        def _():
            arrival(PARTNER, i + 1).wait_recv()

        @pl.when(i + 1 < K)
        def _():
            middle(OWN, i + 1, up, down, p)

        @pl.when(jnp.logical_and(i >= 0, i < mid_near_count))
        def _():
            middle(NEAR, i, near_up, near_down, near_q)

        @pl.when(i + 1 < pairs)
        def _():
            mid_copy(i + 1).start()

        @pl.when(i >= 1)
        def _():
            out_copy(i - 1).start()

        @pl.when(i >= 0)
        def _():
            @pl.when(i < pairs)
            def _():
                mid_copy(i).wait_recv()

            def store(part, value):
                out_buf[i, part] = value

            derivative(
                mid, OWN, up, down, p, i,
                lambda part: rho[OWN, i, part], step_size, store,
            )

    take(K + 1)

    out_copy(K - 1).start()

    @pl.loop(0, N)
    def _(i):
        @pl.when(i < direct_count)
        def _():
            direct_copy(i).wait_send()

        @pl.when(i < pairs)
        def _():
            partner_copy(i).wait_send()
            mid_copy(i).wait_send()

        @pl.when(i < relay_near_count)
        def _():
            relay_near(i).wait_send()

        @pl.when(i < relay_far_count)
        def _():
            relay_far(i).wait_send()

        out_copy(i).wait()


def per_device(hierarchy, hamiltonian, couplings, damp_rates, coef_real, coef_imag):
    total = hierarchy.shape[1]
    M = hierarchy.shape[-1]
    hbm = pl.BlockSpec(memory_space=pltpu.HBM)
    return pl.pallas_call(
        functools.partial(kernel, total, M),
        out_shape=jax.ShapeDtypeStruct(hierarchy.shape, jnp.float32),
        in_specs=[hbm] * 6,
        out_specs=pl.BlockSpec(memory_space=pl.ANY),
        scratch_shapes=[
            pltpu.VMEM((4, total, 2, M, M), jnp.float32),
            pltpu.VMEM((3, total, 2, M, M), jnp.float32),
            pltpu.VMEM((2 * M, 6 * M), jnp.bfloat16),
            pltpu.VMEM((6 * M, 2 * M), jnp.bfloat16),
            pltpu.VMEM((6 * M, 2 * M), jnp.bfloat16),
            pltpu.VMEM((2 * M, 6 * M), jnp.bfloat16),
            pltpu.VMEM((6, total, 8, M), jnp.float32),
            pltpu.VMEM((total, 2, M, M), jnp.float32),
            pltpu.VMEM((3, M, M), jnp.float32),
            pltpu.SMEM(damp_rates.shape, jnp.float32),
            pltpu.SMEM(coef_real.shape, jnp.float32),
            pltpu.SMEM(coef_imag.shape, jnp.float32),
            pltpu.SemaphoreType.DMA((total,)),
            pltpu.SemaphoreType.DMA((total,)),
            pltpu.SemaphoreType.DMA((3,)),
            pltpu.SemaphoreType.DMA((3,)),
            pltpu.SemaphoreType.DMA((5, total)),
            pltpu.SemaphoreType.DMA((4, total)),
        ],
        compiler_params=pltpu.CompilerParams(
            collective_id=0, has_side_effects=True, vmem_limit_bytes=(8 + total) * 2**20
        ),
    )(
        *(
            pltpu.with_memory_space_constraint(x, pltpu.HBM)
            for x in (
                hierarchy,
                hamiltonian,
                couplings,
                damp_rates,
                coef_real,
                coef_imag,
            )
        )
    )


def solution(mesh):
    in_specs = (
        P(("sweep", "na"), None, None, None, None),
        P(),
        P(),
        P("sweep"),
        P("sweep"),
        P("sweep"),
    )
    out_specs = P(("sweep", "na"), None, None, None, None)
    return jax.shard_map(
        per_device, mesh=mesh, in_specs=in_specs, out_specs=out_specs, check_vma=False
    )
```

```python
import functools
import jax
import jax.numpy as jnp
from jax import lax
from jax.experimental import pallas as pl
from jax.experimental.pallas import tpu as pltpu
from jax.sharding import PartitionSpec as P

step_size = 0.02
MESH = pl.DeviceIdType.MESH
NEAR, OWN, PARTNER, FAR = 0, 1, 2, 3
STRIP = 32
LAG = 2


def split(x):
    high = x.astype(jnp.bfloat16)
    return high, (x - high.astype(jnp.float32)).astype(jnp.bfloat16)


def kernel(
    total,
    order,
    hier_ref,
    ham_ref,
    coup_ref,
    damp_in,
    creal_in,
    cimag_in,
    out_ref,
    rho,
    mid,
    w_left,
    w_right,
    x_left,
    x_right,
    table,
    out_buf,
    ham_buf,
    damp_ref,
    creal_ref,
    cimag_ref,
    own_sem,
    out_sem,
    ham_sem,
    small_sem,
    send_sem,
    recv_sem,
):
    M, N = order, total
    p = lax.axis_index("na")
    chip = p // 2
    core = p % 2
    odd = chip % 2
    chips = N // 2
    first = core == 0
    K = N - p
    pairs = N - 1 - 2 * chip

    is_relay = core != odd
    relays = jnp.logical_and(
        is_relay, jnp.where(odd == 1, chip >= 2, chip + 2 < chips)
    )
    fed_by_relay = jnp.logical_and(
        core == odd, jnp.where(odd == 1, chip + 2 < chips, chip >= 2)
    )
    direct_to = jnp.where(odd == 1, 2 * chip - 1, 2 * chip + 2)
    relay_to = jnp.where(odd == 1, p - 3, p + 3)
    relay_from = jnp.where(odd == 1, p + 3, p - 3)

    direct_count = jnp.where(p == 0, K - 2, K)
    near_count = jnp.where(first, jnp.where(p == 0, 0, K + 1), K - 1)
    far_count = jnp.where(
        first,
        jnp.where(
            p == 0, 0, jnp.where(jnp.logical_and(odd == 1, chip >= 2), K + 2, K)
        ),
        jnp.maximum(K - 2, 0),
    )
    relay_near_count = jnp.where(relays, jnp.where(first, near_count, K - 3), 0)
    relay_far_count = jnp.where(relays, far_count, 0)
    mid_near_count = jnp.where(first, jnp.where(p == 0, 0, K), K - 1)
    direct_slot = jnp.where(core == odd, FAR, NEAR)

    def own_copy(i):
        return pltpu.make_async_copy(
            hier_ref.at[0, i], rho.at[OWN, i], own_sem.at[i]
        )

    def operator_copy(k):
        return pltpu.make_async_copy(
            ham_ref if k == 0 else coup_ref.at[k - 1], ham_buf.at[k], ham_sem.at[k]
        )

    def out_copy(i):
        return pltpu.make_async_copy(out_buf.at[i], out_ref.at[0, i], out_sem.at[i])

    def remote(src, dst, send, recv, i, target):
        return pltpu.make_async_remote_copy(
            src_ref=src,
            dst_ref=dst,
            send_sem=send_sem.at[send, i],
            recv_sem=recv_sem.at[recv, i],
            device_id={"na": target},
            device_id_type=MESH,
        )

    def direct_copy(i):
        return remote(
            hier_ref.at[0, i], rho.at[direct_slot, i], 0, direct_slot, i, direct_to
        )

    def partner_copy(i):
        return remote(
            hier_ref.at[0, i], rho.at[PARTNER, i], 1, PARTNER, i, p + 1 - 2 * core
        )

    def relay_near(i):
        return remote(rho.at[NEAR, i], rho.at[FAR, i], 2, FAR, i, relay_to)

    def relay_far(i):
        return remote(rho.at[FAR, i], rho.at[NEAR, i], 3, NEAR, i, relay_to)

    def mid_copy(i):
        return remote(
            mid.at[OWN, i], mid.at[PARTNER, i], 4, 1, i, p + 1 - 2 * core
        )

    def arrival(which, i):
        return remote(
            rho.at[which, i], rho.at[which, i], 0, which, i, p + 1 - 2 * core
        )

    barrier = pltpu.get_barrier_semaphore()

    def greet(target):
        pl.semaphore_signal(
            barrier, inc=1, device_id={"na": target}, device_id_type=MESH
        )

    greet(p + 1 - 2 * core)
    greet(direct_to)

    @pl.when(is_relay)
    def _():
        greet(jnp.where(odd == 1, p - 2, p + 2))

    @pl.when(relays)
    def _():
        greet(relay_to)

    @pl.when(fed_by_relay)
    def _():
        greet(relay_from)

    pl.semaphore_wait(
        barrier,
        2
        + is_relay.astype(jnp.int32)
        + relays.astype(jnp.int32)
        + fed_by_relay.astype(jnp.int32),
    )

    @pl.loop(0, K)
    def _(i):
        @pl.when(i < direct_count)
        def _():
            direct_copy(i).start()

        @pl.when(i < pairs)
        def _():
            partner_copy(i).start()

    small = [
        pltpu.make_async_copy(source, target, small_sem.at[k])
        for k, (source, target) in enumerate(
            ((damp_in, damp_ref), (creal_in, creal_ref), (cimag_in, cimag_ref))
        )
    ]
    for k in range(3):
        small[k].start()
        operator_copy(k).start()

    @pl.loop(0, K)
    def _(i):
        own_copy(i).start()

    for k in range(3):
        operator_copy(k).wait()
        raw = ham_buf[k]
        high, low = split(0.5 * (raw + raw.T))
        for half in range(2):
            cols = slice((3 * half + k) * M, (3 * half + k + 1) * M)
            w_left[0:M, cols] = high
            w_left[M : 2 * M, cols] = low
            w_right[cols, 0:M] = high
            w_right[cols, M : 2 * M] = low

    for copy in small:
        copy.wait()

    for mode in range(2):
        re = jnp.full((8, M), creal_ref[mode], jnp.float32)
        im = jnp.full((8, M), cimag_ref[mode], jnp.float32)
        magnitude = jnp.sqrt(re * re + im * im)

        @pl.loop(0, N)
        def _(n):
            occupied = jnp.full((8, M), n.astype(jnp.float32), jnp.float32)
            lower = jnp.sqrt(occupied / magnitude)
            table[3 * mode, n] = jnp.sqrt((occupied + 1.0) * magnitude)
            table[3 * mode + 1, n] = lower * re
            table[3 * mode + 2, n] = lower * im

    @pl.loop(K, N)
    def _(i):
        out_buf[i] = jnp.zeros((2, M, M), jnp.float32)

    def derivative(buf, own, up, down, q, n, base, scale, store):
        alive = q + n < N - 1
        alive_scale = jnp.where(alive, 1.0, 0.0)
        up = jnp.where(alive, up, own)
        above = jnp.where(alive, n + 1, n)
        below = jnp.maximum(n - 1, 0)
        terms = []
        for mode, occupied in ((0, q), (1, n)):
            terms.append(
                (
                    table[3 * mode, occupied, 0:1, :] * alive_scale,
                    table[3 * mode + 1, occupied, 0:1, :],
                    table[3 * mode + 2, occupied, 0:1, :],
                )
            )
        sources = (((up, n), (down, n)), ((own, above), (own, below)))

        def put(block, rows, part, left, right):
            for x, is_left in ((left, True), (right, False)):
                high, low = split(x)
                for half, value in ((0, high), (1, low)):
                    at = (3 * half + block) * M
                    if is_left:
                        x_left[
                            at + rows : at + rows + STRIP, part * M : (part + 1) * M
                        ] = value
                    else:
                        x_right[
                            part * M + rows : part * M + rows + STRIP, at : at + M
                        ] = value

        for rows in range(0, M, STRIP):
            strip = slice(rows, rows + STRIP)
            for part in range(2):
                high, low = split(buf[own, n, part, strip, :])
                for half, value in ((0, high), (1, low)):
                    at = 3 * half * M
                    x_left[
                        at + rows : at + rows + STRIP, part * M : (part + 1) * M
                    ] = value
                    x_right[
                        part * M + rows : part * M + rows + STRIP, at : at + M
                    ] = value
            for mode in range(2):
                raise_w, direct_w, cross_w = terms[mode]
                (ub, us), (vb, vs) = sources[mode]
                v_re = buf[vb, vs, 0, strip, :]
                v_im = buf[vb, vs, 1, strip, :]
                e_re = raise_w * buf[ub, us, 0, strip, :] + direct_w * v_re
                e_im = raise_w * buf[ub, us, 1, strip, :] + direct_w * v_im
                x_re = cross_w * v_im
                x_im = cross_w * v_re
                put(1 + mode, rows, 0, e_re - x_re, e_re + x_re)
                put(1 + mode, rows, 1, e_im + x_im, e_im - x_im)
        left = jnp.dot(w_left[...], x_left[...], preferred_element_type=jnp.float32)
        right = jnp.dot(x_right[...], w_right[...], preferred_element_type=jnp.float32)
        damping = q.astype(jnp.float32) * damp_ref[0] + n.astype(jnp.float32) * damp_ref[1]
        left = left[0:M] + left[M : 2 * M]
        right = right[:, 0:M] + right[:, M : 2 * M]
        change_re = left[:, M : 2 * M] - right[M : 2 * M] - damping * buf[own, n, 0]
        change_im = right[0:M] - left[:, 0:M] - damping * buf[own, n, 1]
        store(0, base(0) + scale * change_re)
        store(1, base(1) + scale * change_im)

    up = jnp.where(first, PARTNER, NEAR)
    down = jnp.where(first, jnp.where(p == 0, OWN, NEAR), PARTNER)
    near_up = jnp.where(first, OWN, FAR)
    near_down = jnp.where(first, FAR, OWN)
    near_q = jnp.where(first, p - 1, p + 1)

    def take_own(i):
        @pl.when(i < K)
        def _():
            own_copy(i).wait()

    def take(i):
        @pl.when(i < near_count)
        def _():
            arrival(NEAR, i).wait_recv()

        @pl.when(i < relay_near_count)
        def _():
            relay_near(i).start()

        @pl.when(i < far_count)
        def _():
            arrival(FAR, i).wait_recv()

        @pl.when(i < relay_far_count)
        def _():
            relay_far(i).start()

    def middle(which, i, up, down, q):
        def store(part, value):
            mid[which, i, part] = value

        derivative(
            rho, which, up, down, q, i,
            lambda part: rho[which, i, part], 0.5 * step_size, store,
        )

    take_own(jnp.int32(0))

    @pl.loop(K, N)
    def _(i):
        out_copy(i).start()

    @pl.loop(-1, K + LAG)
    def _(i):
        j = i - LAG

        @pl.when(j >= 1)
        def _():
            out_copy(j - 1).start()

        @pl.when(j >= 0)
        def _():
            @pl.when(j < pairs)
            def _():
                mid_copy(j).wait_recv()

            def store(part, value):
                out_buf[j, part] = value

            derivative(
                mid, OWN, up, down, p, j,
                lambda part: rho[OWN, j, part], step_size, store,
            )

        take_own(i + 2)
        take(i + 1)

        @pl.when(i + 1 < pairs)
        def _():
            arrival(PARTNER, i + 1).wait_recv()

        @pl.when(i + 1 < K)
        def _():
            middle(OWN, i + 1, up, down, p)

        @pl.when(jnp.logical_and(i >= 0, i < mid_near_count))
        def _():
            middle(NEAR, i, near_up, near_down, near_q)

        @pl.when(i + 1 < pairs)
        def _():
            mid_copy(i + 1).start()

    out_copy(K - 1).start()

    @pl.loop(0, N)
    def _(i):
        @pl.when(i < direct_count)
        def _():
            direct_copy(i).wait_send()

        @pl.when(i < pairs)
        def _():
            partner_copy(i).wait_send()
            mid_copy(i).wait_send()

        @pl.when(i < relay_near_count)
        def _():
            relay_near(i).wait_send()

        @pl.when(i < relay_far_count)
        def _():
            relay_far(i).wait_send()

        out_copy(i).wait()


def per_device(hierarchy, hamiltonian, couplings, damp_rates, coef_real, coef_imag):
    total = hierarchy.shape[1]
    M = hierarchy.shape[-1]
    hbm = pl.BlockSpec(memory_space=pltpu.HBM)
    return pl.pallas_call(
        functools.partial(kernel, total, M),
        out_shape=jax.ShapeDtypeStruct(hierarchy.shape, jnp.float32),
        in_specs=[hbm] * 6,
        out_specs=pl.BlockSpec(memory_space=pl.ANY),
        scratch_shapes=[
            pltpu.VMEM((4, total, 2, M, M), jnp.float32),
            pltpu.VMEM((3, total, 2, M, M), jnp.float32),
            pltpu.VMEM((2 * M, 6 * M), jnp.bfloat16),
            pltpu.VMEM((6 * M, 2 * M), jnp.bfloat16),
            pltpu.VMEM((6 * M, 2 * M), jnp.bfloat16),
            pltpu.VMEM((2 * M, 6 * M), jnp.bfloat16),
            pltpu.VMEM((6, total, 8, M), jnp.float32),
            pltpu.VMEM((total, 2, M, M), jnp.float32),
            pltpu.VMEM((3, M, M), jnp.float32),
            pltpu.SMEM(damp_rates.shape, jnp.float32),
            pltpu.SMEM(coef_real.shape, jnp.float32),
            pltpu.SMEM(coef_imag.shape, jnp.float32),
            pltpu.SemaphoreType.DMA((total,)),
            pltpu.SemaphoreType.DMA((total,)),
            pltpu.SemaphoreType.DMA((3,)),
            pltpu.SemaphoreType.DMA((3,)),
            pltpu.SemaphoreType.DMA((5, total)),
            pltpu.SemaphoreType.DMA((4, total)),
        ],
        compiler_params=pltpu.CompilerParams(
            collective_id=0, has_side_effects=True, vmem_limit_bytes=(8 + total) * 2**20
        ),
    )(
        *(
            pltpu.with_memory_space_constraint(x, pltpu.HBM)
            for x in (
                hierarchy,
                hamiltonian,
                couplings,
                damp_rates,
                coef_real,
                coef_imag,
            )
        )
    )


def solution(mesh):
    in_specs = (
        P(("sweep", "na"), None, None, None, None),
        P(),
        P(),
        P("sweep"),
        P("sweep"),
        P("sweep"),
    )
    out_specs = P(("sweep", "na"), None, None, None, None)
    return jax.shard_map(
        per_device, mesh=mesh, in_specs=in_specs, out_specs=out_specs, check_vma=False
    )
```

```python
import functools
import jax
import jax.numpy as jnp
from jax import lax
from jax.experimental import pallas as pl
from jax.experimental.pallas import tpu as pltpu
from jax.sharding import PartitionSpec as P

step_size = 0.02
MESH = pl.DeviceIdType.MESH
NEAR, OWN, PARTNER, FAR = 0, 1, 2, 3
STRIP = 32
LAG = 2
EARLY = 3


def split(x):
    high = x.astype(jnp.bfloat16)
    return high, (x - high.astype(jnp.float32)).astype(jnp.bfloat16)


def kernel(
    total,
    order,
    hier_ref,
    ham_ref,
    coup_ref,
    damp_in,
    creal_in,
    cimag_in,
    out_ref,
    rho,
    mid,
    w_left,
    w_right,
    x_left,
    x_right,
    table,
    out_buf,
    ham_buf,
    damp_ref,
    creal_ref,
    cimag_ref,
    own_sem,
    out_sem,
    ham_sem,
    small_sem,
    send_sem,
    recv_sem,
):
    M, N = order, total
    p = lax.axis_index("na")
    chip = p // 2
    core = p % 2
    odd = chip % 2
    chips = N // 2
    first = core == 0
    K = N - p
    pairs = N - 1 - 2 * chip

    is_relay = core != odd
    relays = jnp.logical_and(
        is_relay, jnp.where(odd == 1, chip >= 2, chip + 2 < chips)
    )
    fed_by_relay = jnp.logical_and(
        core == odd, jnp.where(odd == 1, chip + 2 < chips, chip >= 2)
    )
    direct_to = jnp.where(odd == 1, 2 * chip - 1, 2 * chip + 2)
    relay_to = jnp.where(odd == 1, p - 3, p + 3)
    relay_from = jnp.where(odd == 1, p + 3, p - 3)

    direct_count = jnp.where(p == 0, K - 2, K)
    near_count = jnp.where(first, jnp.where(p == 0, 0, K + 1), K - 1)
    far_count = jnp.where(
        first,
        jnp.where(
            p == 0, 0, jnp.where(jnp.logical_and(odd == 1, chip >= 2), K + 2, K)
        ),
        jnp.maximum(K - 2, 0),
    )
    relay_near_count = jnp.where(relays, jnp.where(first, near_count, K - 3), 0)
    relay_far_count = jnp.where(relays, far_count, 0)
    mid_near_count = jnp.where(first, jnp.where(p == 0, 0, K), K - 1)
    direct_slot = jnp.where(core == odd, FAR, NEAR)

    def own_copy(i):
        return pltpu.make_async_copy(
            hier_ref.at[0, i], rho.at[OWN, i], own_sem.at[i]
        )

    def operator_copy(k):
        return pltpu.make_async_copy(
            ham_ref if k == 0 else coup_ref.at[k - 1], ham_buf.at[k], ham_sem.at[k]
        )

    def out_copy(i):
        return pltpu.make_async_copy(out_buf.at[i], out_ref.at[0, i], out_sem.at[i])

    def remote(src, dst, send, recv, i, target):
        return pltpu.make_async_remote_copy(
            src_ref=src,
            dst_ref=dst,
            send_sem=send_sem.at[send, i],
            recv_sem=recv_sem.at[recv, i],
            device_id={"na": target},
            device_id_type=MESH,
        )

    def direct_copy(i):
        return remote(
            hier_ref.at[0, i], rho.at[direct_slot, i], 0, direct_slot, i, direct_to
        )

    def partner_copy(i):
        return remote(
            hier_ref.at[0, i], rho.at[PARTNER, i], 1, PARTNER, i, p + 1 - 2 * core
        )

    def relay_near(i):
        return remote(rho.at[NEAR, i], rho.at[FAR, i], 2, FAR, i, relay_to)

    def relay_far(i):
        return remote(rho.at[FAR, i], rho.at[NEAR, i], 3, NEAR, i, relay_to)

    def mid_copy(i):
        return remote(
            mid.at[OWN, i], mid.at[PARTNER, i], 4, 1, i, p + 1 - 2 * core
        )

    def arrival(which, i):
        return remote(
            rho.at[which, i], rho.at[which, i], 0, which, i, p + 1 - 2 * core
        )

    barrier = pltpu.get_barrier_semaphore()

    def greet(target):
        pl.semaphore_signal(
            barrier, inc=1, device_id={"na": target}, device_id_type=MESH
        )

    greet(p + 1 - 2 * core)
    greet(direct_to)

    @pl.when(is_relay)
    def _():
        greet(jnp.where(odd == 1, p - 2, p + 2))

    @pl.when(relays)
    def _():
        greet(relay_to)

    @pl.when(fed_by_relay)
    def _():
        greet(relay_from)

    pl.semaphore_wait(
        barrier,
        2
        + is_relay.astype(jnp.int32)
        + relays.astype(jnp.int32)
        + fed_by_relay.astype(jnp.int32),
    )

    @pl.loop(0, K)
    def _(i):
        @pl.when(i < direct_count)
        def _():
            direct_copy(i).start()

        @pl.when(i < pairs)
        def _():
            partner_copy(i).start()

    small = [
        pltpu.make_async_copy(source, target, small_sem.at[k])
        for k, (source, target) in enumerate(
            ((damp_in, damp_ref), (creal_in, creal_ref), (cimag_in, cimag_ref))
        )
    ]
    for k in range(3):
        small[k].start()
        operator_copy(k).start()

    @pl.loop(0, K)
    def _(i):
        own_copy(i).start()

    for k in range(3):
        operator_copy(k).wait()
        raw = ham_buf[k]
        high, low = split(0.5 * (raw + raw.T))
        for half in range(2):
            cols = slice((3 * half + k) * M, (3 * half + k + 1) * M)
            w_left[0:M, cols] = high
            w_left[M : 2 * M, cols] = low
            w_right[cols, 0:M] = high
            w_right[cols, M : 2 * M] = low

    for copy in small:
        copy.wait()

    for mode in range(2):
        re = jnp.full((8, M), creal_ref[mode], jnp.float32)
        im = jnp.full((8, M), cimag_ref[mode], jnp.float32)
        magnitude = jnp.sqrt(re * re + im * im)

        @pl.loop(0, N)
        def _(n):
            occupied = jnp.full((8, M), n.astype(jnp.float32), jnp.float32)
            lower = jnp.sqrt(occupied / magnitude)
            table[3 * mode, n] = jnp.sqrt((occupied + 1.0) * magnitude)
            table[3 * mode + 1, n] = lower * re
            table[3 * mode + 2, n] = lower * im

    @pl.loop(K, N)
    def _(i):
        out_buf[i] = jnp.zeros((2, M, M), jnp.float32)

    def derivative(buf, own, up, down, q, n, base, scale, store):
        alive = q + n < N - 1
        alive_scale = jnp.where(alive, 1.0, 0.0)
        up = jnp.where(alive, up, own)
        above = jnp.where(alive, n + 1, n)
        below = jnp.maximum(n - 1, 0)
        terms = []
        for mode, occupied in ((0, q), (1, n)):
            terms.append(
                (
                    table[3 * mode, occupied, 0:1, :] * alive_scale,
                    table[3 * mode + 1, occupied, 0:1, :],
                    table[3 * mode + 2, occupied, 0:1, :],
                )
            )
        sources = (((up, n), (down, n)), ((own, above), (own, below)))

        def put(block, rows, part, left, right):
            for x, is_left in ((left, True), (right, False)):
                high, low = split(x)
                for half, value in ((0, high), (1, low)):
                    at = (3 * half + block) * M
                    if is_left:
                        x_left[
                            at + rows : at + rows + STRIP, part * M : (part + 1) * M
                        ] = value
                    else:
                        x_right[
                            part * M + rows : part * M + rows + STRIP, at : at + M
                        ] = value

        for rows in range(0, M, STRIP):
            strip = slice(rows, rows + STRIP)
            for part in range(2):
                high, low = split(buf[own, n, part, strip, :])
                for half, value in ((0, high), (1, low)):
                    at = 3 * half * M
                    x_left[
                        at + rows : at + rows + STRIP, part * M : (part + 1) * M
                    ] = value
                    x_right[
                        part * M + rows : part * M + rows + STRIP, at : at + M
                    ] = value
            for mode in range(2):
                raise_w, direct_w, cross_w = terms[mode]
                (ub, us), (vb, vs) = sources[mode]
                v_re = buf[vb, vs, 0, strip, :]
                v_im = buf[vb, vs, 1, strip, :]
                e_re = raise_w * buf[ub, us, 0, strip, :] + direct_w * v_re
                e_im = raise_w * buf[ub, us, 1, strip, :] + direct_w * v_im
                x_re = cross_w * v_im
                x_im = cross_w * v_re
                put(1 + mode, rows, 0, e_re - x_re, e_re + x_re)
                put(1 + mode, rows, 1, e_im + x_im, e_im - x_im)
        left = jnp.dot(w_left[...], x_left[...], preferred_element_type=jnp.float32)
        right = jnp.dot(x_right[...], w_right[...], preferred_element_type=jnp.float32)
        damping = q.astype(jnp.float32) * damp_ref[0] + n.astype(jnp.float32) * damp_ref[1]
        left = left[0:M] + left[M : 2 * M]
        right = right[:, 0:M] + right[:, M : 2 * M]
        change_re = left[:, M : 2 * M] - right[M : 2 * M] - damping * buf[own, n, 0]
        change_im = right[0:M] - left[:, 0:M] - damping * buf[own, n, 1]
        store(0, base(0) + scale * change_re)
        store(1, base(1) + scale * change_im)

    up = jnp.where(first, PARTNER, NEAR)
    down = jnp.where(first, jnp.where(p == 0, OWN, NEAR), PARTNER)
    near_up = jnp.where(first, OWN, FAR)
    near_down = jnp.where(first, FAR, OWN)
    near_q = jnp.where(first, p - 1, p + 1)

    def take(i):
        @pl.when(i < near_count)
        def _():
            arrival(NEAR, i).wait_recv()

        @pl.when(i < relay_near_count)
        def _():
            relay_near(i).start()

        @pl.when(i < far_count)
        def _():
            arrival(FAR, i).wait_recv()

        @pl.when(i < relay_far_count)
        def _():
            relay_far(i).start()

    def middle(which, i, up, down, q):
        def store(part, value):
            mid[which, i, part] = value

        derivative(
            rho, which, up, down, q, i,
            lambda part: rho[which, i, part], 0.5 * step_size, store,
        )

    early = jnp.logical_and(core == 1, K - 1 > EARLY + 1)
    in_turn = jnp.where(early, K - 1, K)

    @pl.loop(0, K)
    def _(i):
        own_copy(i).wait()


    @pl.loop(K, N)
    def _(i):
        out_copy(i).start()

    @pl.loop(-1, K + LAG)
    def _(i):
        j = i - LAG

        @pl.when(j >= 1)
        def _():
            out_copy(j - 1).start()

        @pl.when(j >= 0)
        def _():
            @pl.when(j < pairs)
            def _():
                mid_copy(j).wait_recv()

            def store(part, value):
                out_buf[j, part] = value

            derivative(
                mid, OWN, up, down, p, j,
                lambda part: rho[OWN, j, part], step_size, store,
            )

        take(i + 1)

        @pl.when(jnp.logical_and(i < EARLY, i + 1 < pairs))
        def _():
            arrival(PARTNER, i + 1).wait_recv()

        @pl.when(i == EARLY)
        def _():
            @pl.loop(EARLY + 1, pairs)
            def _(k):
                arrival(PARTNER, k).wait_recv()

        @pl.when(i + 1 < in_turn)
        def _():
            middle(OWN, i + 1, up, down, p)

        @pl.when(jnp.logical_and(early, i == EARLY))
        def _():
            middle(OWN, K - 1, up, down, p)

        @pl.when(jnp.logical_and(i >= 0, i < mid_near_count))
        def _():
            middle(NEAR, i, near_up, near_down, near_q)

        @pl.when(jnp.logical_and(i + 1 < pairs, i + 1 < in_turn))
        def _():
            mid_copy(i + 1).start()

        @pl.when(jnp.logical_and(early, i == EARLY))
        def _():
            mid_copy(K - 1).start()

    out_copy(K - 1).start()

    @pl.loop(0, N)
    def _(i):
        @pl.when(i < direct_count)
        def _():
            direct_copy(i).wait_send()

        @pl.when(i < pairs)
        def _():
            partner_copy(i).wait_send()
            mid_copy(i).wait_send()

        @pl.when(i < relay_near_count)
        def _():
            relay_near(i).wait_send()

        @pl.when(i < relay_far_count)
        def _():
            relay_far(i).wait_send()

        out_copy(i).wait()


def per_device(hierarchy, hamiltonian, couplings, damp_rates, coef_real, coef_imag):
    total = hierarchy.shape[1]
    M = hierarchy.shape[-1]
    hbm = pl.BlockSpec(memory_space=pltpu.HBM)
    return pl.pallas_call(
        functools.partial(kernel, total, M),
        out_shape=jax.ShapeDtypeStruct(hierarchy.shape, jnp.float32),
        in_specs=[hbm] * 6,
        out_specs=pl.BlockSpec(memory_space=pl.ANY),
        scratch_shapes=[
            pltpu.VMEM((4, total, 2, M, M), jnp.float32),
            pltpu.VMEM((3, total, 2, M, M), jnp.float32),
            pltpu.VMEM((2 * M, 6 * M), jnp.bfloat16),
            pltpu.VMEM((6 * M, 2 * M), jnp.bfloat16),
            pltpu.VMEM((6 * M, 2 * M), jnp.bfloat16),
            pltpu.VMEM((2 * M, 6 * M), jnp.bfloat16),
            pltpu.VMEM((6, total, 8, M), jnp.float32),
            pltpu.VMEM((total, 2, M, M), jnp.float32),
            pltpu.VMEM((3, M, M), jnp.float32),
            pltpu.SMEM(damp_rates.shape, jnp.float32),
            pltpu.SMEM(coef_real.shape, jnp.float32),
            pltpu.SMEM(coef_imag.shape, jnp.float32),
            pltpu.SemaphoreType.DMA((total,)),
            pltpu.SemaphoreType.DMA((total,)),
            pltpu.SemaphoreType.DMA((3,)),
            pltpu.SemaphoreType.DMA((3,)),
            pltpu.SemaphoreType.DMA((5, total)),
            pltpu.SemaphoreType.DMA((4, total)),
        ],
        compiler_params=pltpu.CompilerParams(
            collective_id=0, has_side_effects=True, vmem_limit_bytes=(8 + total) * 2**20
        ),
    )(
        *(
            pltpu.with_memory_space_constraint(x, pltpu.HBM)
            for x in (
                hierarchy,
                hamiltonian,
                couplings,
                damp_rates,
                coef_real,
                coef_imag,
            )
        )
    )


def solution(mesh):
    in_specs = (
        P(("sweep", "na"), None, None, None, None),
        P(),
        P(),
        P("sweep"),
        P("sweep"),
        P("sweep"),
    )
    out_specs = P(("sweep", "na"), None, None, None, None)
    return jax.shard_map(
        per_device, mesh=mesh, in_specs=in_specs, out_specs=out_specs, check_vma=False
    )
```

```python
import functools
import jax
import jax.numpy as jnp
from jax import lax
from jax.experimental import pallas as pl
from jax.experimental.pallas import tpu as pltpu
from jax.sharding import PartitionSpec as P

step_size = 0.02
MESH = pl.DeviceIdType.MESH
NEAR, OWN, PARTNER, FAR = 0, 1, 2, 3
STRIP = 32
LAG = 2
EARLY = 3


def split(x):
    high = x.astype(jnp.bfloat16)
    return high, (x - high.astype(jnp.float32)).astype(jnp.bfloat16)


def kernel(
    total,
    order,
    hier_ref,
    ham_ref,
    coup_ref,
    damp_in,
    creal_in,
    cimag_in,
    out_ref,
    rho,
    mid,
    w_left,
    w_right,
    x_left,
    x_right,
    table,
    out_buf,
    ham_buf,
    damp_ref,
    creal_ref,
    cimag_ref,
    own_sem,
    out_sem,
    ham_sem,
    small_sem,
    send_sem,
    recv_sem,
):
    M, N = order, total
    p = lax.axis_index("na")
    chip = p // 2
    core = p % 2
    odd = chip % 2
    chips = N // 2
    first = core == 0
    K = N - p
    pairs = N - 1 - 2 * chip

    is_relay = core != odd
    relays = jnp.logical_and(
        is_relay, jnp.where(odd == 1, chip >= 2, chip + 2 < chips)
    )
    fed_by_relay = jnp.logical_and(
        core == odd, jnp.where(odd == 1, chip + 2 < chips, chip >= 2)
    )
    direct_to = jnp.where(odd == 1, 2 * chip - 1, 2 * chip + 2)
    relay_to = jnp.where(odd == 1, p - 3, p + 3)
    relay_from = jnp.where(odd == 1, p + 3, p - 3)

    direct_count = jnp.where(p == 0, K - 2, K)
    near_count = jnp.where(first, jnp.where(p == 0, 0, K + 1), K - 1)
    far_count = jnp.where(
        first,
        jnp.where(
            p == 0, 0, jnp.where(jnp.logical_and(odd == 1, chip >= 2), K + 2, K)
        ),
        jnp.maximum(K - 2, 0),
    )
    relay_near_count = jnp.where(relays, jnp.where(first, near_count, K - 3), 0)
    relay_far_count = jnp.where(relays, far_count, 0)
    mid_near_count = jnp.where(first, jnp.where(p == 0, 0, K), K - 1)
    direct_slot = jnp.where(core == odd, FAR, NEAR)

    def own_copy(i):
        return pltpu.make_async_copy(
            hier_ref.at[0, i], rho.at[OWN, i], own_sem.at[i]
        )

    def operator_copy(k):
        return pltpu.make_async_copy(
            ham_ref if k == 0 else coup_ref.at[k - 1], ham_buf.at[k], ham_sem.at[k]
        )

    def out_copy(i):
        return pltpu.make_async_copy(out_buf.at[i], out_ref.at[0, i], out_sem.at[i])

    def remote(src, dst, send, recv, i, target):
        return pltpu.make_async_remote_copy(
            src_ref=src,
            dst_ref=dst,
            send_sem=send_sem.at[send, i],
            recv_sem=recv_sem.at[recv, i],
            device_id={"na": target},
            device_id_type=MESH,
        )

    def direct_copy(i):
        return remote(
            hier_ref.at[0, i], rho.at[direct_slot, i], 0, direct_slot, i, direct_to
        )

    def partner_copy(i):
        return remote(
            hier_ref.at[0, i], rho.at[PARTNER, i], 1, PARTNER, i, p + 1 - 2 * core
        )

    def relay_near(i):
        return remote(rho.at[NEAR, i], rho.at[FAR, i], 2, FAR, i, relay_to)

    def relay_far(i):
        return remote(rho.at[FAR, i], rho.at[NEAR, i], 3, NEAR, i, relay_to)

    def mid_copy(i):
        return remote(
            mid.at[OWN, i], mid.at[PARTNER, i], 4, 1, i, p + 1 - 2 * core
        )

    def arrival(which, i):
        return remote(
            rho.at[which, i], rho.at[which, i], 0, which, i, p + 1 - 2 * core
        )

    barrier = pltpu.get_barrier_semaphore()

    def greet(target):
        pl.semaphore_signal(
            barrier, inc=1, device_id={"na": target}, device_id_type=MESH
        )

    greet(p + 1 - 2 * core)
    greet(direct_to)

    @pl.when(is_relay)
    def _():
        greet(jnp.where(odd == 1, p - 2, p + 2))

    @pl.when(relays)
    def _():
        greet(relay_to)

    @pl.when(fed_by_relay)
    def _():
        greet(relay_from)

    pl.semaphore_wait(
        barrier,
        2
        + is_relay.astype(jnp.int32)
        + relays.astype(jnp.int32)
        + fed_by_relay.astype(jnp.int32),
    )

    @pl.loop(0, K)
    def _(i):
        @pl.when(i < direct_count)
        def _():
            direct_copy(i).start()

        @pl.when(i < pairs)
        def _():
            partner_copy(i).start()

    small = [
        pltpu.make_async_copy(source, target, small_sem.at[k])
        for k, (source, target) in enumerate(
            ((damp_in, damp_ref), (creal_in, creal_ref), (cimag_in, cimag_ref))
        )
    ]
    for k in range(3):
        small[k].start()
        operator_copy(k).start()

    @pl.loop(0, K)
    def _(i):
        own_copy(i).start()

    for k in range(3):
        operator_copy(k).wait()
        raw = ham_buf[k]
        high, low = split(0.5 * (raw + raw.T))
        for half in range(2):
            cols = slice((3 * half + k) * M, (3 * half + k + 1) * M)
            w_left[0:M, cols] = high
            w_left[M : 2 * M, cols] = low
            w_right[cols, 0:M] = high
            w_right[cols, M : 2 * M] = low

    for copy in small:
        copy.wait()

    for mode in range(2):
        re = jnp.full((8, M), creal_ref[mode], jnp.float32)
        im = jnp.full((8, M), cimag_ref[mode], jnp.float32)
        magnitude = jnp.sqrt(re * re + im * im)

        @pl.loop(0, N)
        def _(n):
            occupied = jnp.full((8, M), n.astype(jnp.float32), jnp.float32)
            lower = jnp.sqrt(occupied / magnitude)
            table[3 * mode, n] = jnp.sqrt((occupied + 1.0) * magnitude)
            table[3 * mode + 1, n] = lower * re
            table[3 * mode + 2, n] = lower * im

    @pl.loop(K, N)
    def _(i):
        out_buf[i] = jnp.zeros((2, M, M), jnp.float32)

    def derivative(buf, own, up, down, q, n, base, scale, store):
        alive = q + n < N - 1
        alive_scale = jnp.where(alive, 1.0, 0.0)
        up = jnp.where(alive, up, own)
        above = jnp.where(alive, n + 1, n)
        below = jnp.maximum(n - 1, 0)
        terms = []
        for mode, occupied in ((0, q), (1, n)):
            terms.append(
                (
                    table[3 * mode, occupied, 0:1, :] * alive_scale,
                    table[3 * mode + 1, occupied, 0:1, :],
                    table[3 * mode + 2, occupied, 0:1, :],
                )
            )
        sources = (((up, n), (down, n)), ((own, above), (own, below)))

        def put(block, rows, part, left, right):
            for x, is_left in ((left, True), (right, False)):
                high, low = split(x)
                for half, value in ((0, high), (1, low)):
                    at = (3 * half + block) * M
                    if is_left:
                        x_left[
                            at + rows : at + rows + STRIP, part * M : (part + 1) * M
                        ] = value
                    else:
                        x_right[
                            part * M + rows : part * M + rows + STRIP, at : at + M
                        ] = value

        for rows in range(0, M, STRIP):
            strip = slice(rows, rows + STRIP)
            for part in range(2):
                high, low = split(buf[own, n, part, strip, :])
                for half, value in ((0, high), (1, low)):
                    at = 3 * half * M
                    x_left[
                        at + rows : at + rows + STRIP, part * M : (part + 1) * M
                    ] = value
                    x_right[
                        part * M + rows : part * M + rows + STRIP, at : at + M
                    ] = value
            for mode in range(2):
                raise_w, direct_w, cross_w = terms[mode]
                (ub, us), (vb, vs) = sources[mode]
                v_re = buf[vb, vs, 0, strip, :]
                v_im = buf[vb, vs, 1, strip, :]
                e_re = raise_w * buf[ub, us, 0, strip, :] + direct_w * v_re
                e_im = raise_w * buf[ub, us, 1, strip, :] + direct_w * v_im
                x_re = cross_w * v_im
                x_im = cross_w * v_re
                put(1 + mode, rows, 0, e_re - x_re, e_re + x_re)
                put(1 + mode, rows, 1, e_im + x_im, e_im - x_im)
        left = jnp.dot(w_left[...], x_left[...], preferred_element_type=jnp.float32)
        right = jnp.dot(x_right[...], w_right[...], preferred_element_type=jnp.float32)
        damping = q.astype(jnp.float32) * damp_ref[0] + n.astype(jnp.float32) * damp_ref[1]
        left = left[0:M] + left[M : 2 * M]
        right = right[:, 0:M] + right[:, M : 2 * M]
        change_re = left[:, M : 2 * M] - right[M : 2 * M] - damping * buf[own, n, 0]
        change_im = right[0:M] - left[:, 0:M] - damping * buf[own, n, 1]
        store(0, base(0) + scale * change_re)
        store(1, base(1) + scale * change_im)

    up = jnp.where(first, PARTNER, NEAR)
    down = jnp.where(first, jnp.where(p == 0, OWN, NEAR), PARTNER)
    near_up = jnp.where(first, OWN, FAR)
    near_down = jnp.where(first, FAR, OWN)
    near_q = jnp.where(first, p - 1, p + 1)

    def take(i):
        @pl.when(i < near_count)
        def _():
            arrival(NEAR, i).wait_recv()

        @pl.when(i < relay_near_count)
        def _():
            relay_near(i).start()

        @pl.when(i < far_count)
        def _():
            arrival(FAR, i).wait_recv()

        @pl.when(i < relay_far_count)
        def _():
            relay_far(i).start()

    def middle(which, i, up, down, q):
        def store(part, value):
            mid[which, i, part] = value

        derivative(
            rho, which, up, down, q, i,
            lambda part: rho[which, i, part], 0.5 * step_size, store,
        )

    early = jnp.logical_and(core == 1, K - 1 > EARLY + 1)
    in_turn = jnp.where(early, K - 1, K)

    @pl.loop(0, K)
    def _(i):
        own_copy(i).wait()


    @pl.loop(K, N)
    def _(i):
        out_copy(i).start()

    lag = jnp.where(p == 1, 1, LAG)

    @pl.loop(-1, K + lag)
    def _(i):
        j = i - lag

        @pl.when(j >= 1)
        def _():
            out_copy(j - 1).start()

        @pl.when(j >= 0)
        def _():
            @pl.when(j < pairs)
            def _():
                mid_copy(j).wait_recv()

            def store(part, value):
                out_buf[j, part] = value

            derivative(
                mid, OWN, up, down, p, j,
                lambda part: rho[OWN, j, part], step_size, store,
            )

        take(i + 1)

        @pl.when(jnp.logical_and(i < EARLY, i + 1 < pairs))
        def _():
            arrival(PARTNER, i + 1).wait_recv()

        @pl.when(i == EARLY)
        def _():
            @pl.loop(EARLY + 1, pairs)
            def _(k):
                arrival(PARTNER, k).wait_recv()

        @pl.when(i + 1 < in_turn)
        def _():
            middle(OWN, i + 1, up, down, p)

        @pl.when(jnp.logical_and(early, i == EARLY))
        def _():
            middle(OWN, K - 1, up, down, p)

        @pl.when(jnp.logical_and(i >= 0, i < mid_near_count))
        def _():
            middle(NEAR, i, near_up, near_down, near_q)

        @pl.when(jnp.logical_and(i + 1 < pairs, i + 1 < in_turn))
        def _():
            mid_copy(i + 1).start()

        @pl.when(jnp.logical_and(early, i == EARLY))
        def _():
            mid_copy(K - 1).start()

    out_copy(K - 1).start()

    @pl.loop(0, N)
    def _(i):
        @pl.when(i < direct_count)
        def _():
            direct_copy(i).wait_send()

        @pl.when(i < pairs)
        def _():
            partner_copy(i).wait_send()
            mid_copy(i).wait_send()

        @pl.when(i < relay_near_count)
        def _():
            relay_near(i).wait_send()

        @pl.when(i < relay_far_count)
        def _():
            relay_far(i).wait_send()

        out_copy(i).wait()


def per_device(hierarchy, hamiltonian, couplings, damp_rates, coef_real, coef_imag):
    total = hierarchy.shape[1]
    M = hierarchy.shape[-1]
    hbm = pl.BlockSpec(memory_space=pltpu.HBM)
    return pl.pallas_call(
        functools.partial(kernel, total, M),
        out_shape=jax.ShapeDtypeStruct(hierarchy.shape, jnp.float32),
        in_specs=[hbm] * 6,
        out_specs=pl.BlockSpec(memory_space=pl.ANY),
        scratch_shapes=[
            pltpu.VMEM((4, total, 2, M, M), jnp.float32),
            pltpu.VMEM((3, total, 2, M, M), jnp.float32),
            pltpu.VMEM((2 * M, 6 * M), jnp.bfloat16),
            pltpu.VMEM((6 * M, 2 * M), jnp.bfloat16),
            pltpu.VMEM((6 * M, 2 * M), jnp.bfloat16),
            pltpu.VMEM((2 * M, 6 * M), jnp.bfloat16),
            pltpu.VMEM((6, total, 8, M), jnp.float32),
            pltpu.VMEM((total, 2, M, M), jnp.float32),
            pltpu.VMEM((3, M, M), jnp.float32),
            pltpu.SMEM(damp_rates.shape, jnp.float32),
            pltpu.SMEM(coef_real.shape, jnp.float32),
            pltpu.SMEM(coef_imag.shape, jnp.float32),
            pltpu.SemaphoreType.DMA((total,)),
            pltpu.SemaphoreType.DMA((total,)),
            pltpu.SemaphoreType.DMA((3,)),
            pltpu.SemaphoreType.DMA((3,)),
            pltpu.SemaphoreType.DMA((5, total)),
            pltpu.SemaphoreType.DMA((4, total)),
        ],
        compiler_params=pltpu.CompilerParams(
            collective_id=0, has_side_effects=True, vmem_limit_bytes=(8 + total) * 2**20
        ),
    )(
        *(
            pltpu.with_memory_space_constraint(x, pltpu.HBM)
            for x in (
                hierarchy,
                hamiltonian,
                couplings,
                damp_rates,
                coef_real,
                coef_imag,
            )
        )
    )


def solution(mesh):
    in_specs = (
        P(("sweep", "na"), None, None, None, None),
        P(),
        P(),
        P("sweep"),
        P("sweep"),
        P("sweep"),
    )
    out_specs = P(("sweep", "na"), None, None, None, None)
    return jax.shard_map(
        per_device, mesh=mesh, in_specs=in_specs, out_specs=out_specs, check_vma=False
    )
```
